32 devices in a mesh: design: 2 (over y), layer: 4 (over z), harm: 4 (over x, core).
Axes of the slice: x: 2, y: 2, z: 4, core: 2. Of those that a mesh axis runs over, the one named last changes fastest.
Arguments:
- incident: float32 [2048, 512], P(('design', 'harm')), parts along dimension 0, may hold values from -6 to 6
- target: float32 [2048, 512], P(('design', 'harm')), parts along dimension 0, may hold values from -6 to 6
- down_diag: float32 [16, 1024, 128], P(('design', 'layer'), 'harm'), parts along dimension 0, may hold values from -0.375 to 0.375
- down_off: float32 [16, 1024, 128], P(('design', 'layer'), 'harm'), parts along dimension 0, may hold values from -0.375 to 0.375
- up_diag: float32 [16, 1024, 128], P(('design', 'layer'), 'harm'), parts along dimension 0, may hold values from -0.375 to 0.375
- up_off: float32 [16, 1024, 128], P(('design', 'layer'), 'harm'), parts along dimension 0, may hold values from -0.375 to 0.375
- design: float32 [16, 1024], P(('design', 'layer'), 'harm'), parts along dimension 0, may hold values from -0.5 to 0.5
- profile: float32 [16, 1024], replicated, may hold values from 0.25 to 1
- material: int32 [16], P(('design', 'layer')), parts along dimension 0, may hold values from 0 to 15
- offsets: int32 [16], P(('design', 'layer')), parts along dimension 0, may hold values from 1 to 7
Outputs:
- gradient: float32 [16, 1024], P(('design', 'layer'), 'harm'), parts along dimension 0
The draws below stay inside these ranges and needn't reach their ends.
There are 2 independent parts, one for each index of `design`. The reference program is written for one: setup_inputs(seed, part) draws one part's arguments, and reference() takes and returns one part's arrays. A program takes and returns all parts, laid end to end along the dimension named above; an argument that names none is the same for every part. Nothing has to cross between parts.
All inputs are finite; a program needn't handle non-finite values.
Results may differ from the reference program's by a relative error of at most 0.00028.
Values sent between devices are 32-bit elements; how exact they have to be, the bound alone decides.
No kernel may reach another device: no remote copies, remote signals or barrier semaphores. Data moves between devices by JAX's collectives and lax.ppermute only.
A program may use at most 64 MiB of HBM per device.

```python
import math
import jax
import jax.numpy as jnp
from jax import lax

HARM = 1024
BLK = 128
NB = 8
MATS = 16
LAYERS = 8
NIN = 512


def touch_ends(values, rng, smallest, largest):
    extent = values.shape
    spot = [jax.random.randint(jax.random.fold_in(rng, axis), (), 0, extent[axis]) for axis in range(len(extent))]
    values = values.at[tuple(spot)].set(smallest)
    longest = extent.index(max(extent))
    spot[longest] = (spot[longest] + 1) % extent[longest]
    return values.at[tuple(spot)].set(largest)


def levels(stream_key, extent, split, low, top_value):
    factor_of, own = 1.0, jax.random.fold_in(stream_key, 6)
    for dim, shards_of in split:
        steps = jnp.exp(jax.random.uniform(jax.random.fold_in(own, dim), (shards_of,), jnp.float32, low / len(split), top_value / len(split)))
        factor_of = factor_of * jnp.repeat(steps, extent[dim] // shards_of).reshape([-1 if axis == dim else 1 for axis in range(len(extent))])
    return factor_of


def gaussian(key, extent, width, bound, cuts=(), kind=jnp.bfloat16):
    level = levels(key, extent, cuts, -0.22, 0.18) if cuts else 1.0
    drawn = jax.random.normal(key, extent, jnp.float32) * width * level
    return jnp.minimum(jnp.maximum(drawn, -bound), bound).astype(kind)


def setup_inputs(seed: int = 0, part: int = 0) -> dict:
    seeds = jax.random.split(jax.random.key(seed), 11)
    part_keys = jax.random.split(jax.random.fold_in(seeds[10], part), 11)
    incident = gaussian(part_keys[0], (HARM, NIN), 1.0, 6.0, ((0, 4),), jnp.float32)
    target = gaussian(part_keys[1], (HARM, NIN), 1.0, 6.0, ((0, 4),), jnp.float32)
    down_diag = gaussian(part_keys[2], (LAYERS, HARM, BLK), (2 * BLK) ** -0.5, 0.375, ((0, 4), (1, 4)), jnp.float32)
    down_off = gaussian(part_keys[3], (LAYERS, HARM, BLK), (2 * BLK) ** -0.5, 0.375, ((0, 4), (1, 4)), jnp.float32)
    up_diag = gaussian(part_keys[4], (LAYERS, HARM, BLK), (2 * BLK) ** -0.5, 0.375, ((0, 4), (1, 4)), jnp.float32)
    up_off = gaussian(part_keys[5], (LAYERS, HARM, BLK), (2 * BLK) ** -0.5, 0.375, ((0, 4), (1, 4)), jnp.float32)
    design = jnp.clip(jax.random.uniform(part_keys[6], (LAYERS, HARM), jnp.float32, -0.5, 0.5) * levels(part_keys[6], (LAYERS, HARM), ((0, 4), (1, 4)), -0.4, 0.0), -0.5, 0.5)
    profile = jnp.clip(jnp.exp(jax.random.uniform(seeds[7], (MATS, HARM), jnp.float32, math.log(0.25), math.log(1.0))), 0.25, 1.0)
    material = touch_ends(jax.random.randint(part_keys[8], (LAYERS,), 0, MATS), jax.random.fold_in(part_keys[8], 1), 0, MATS - 1).astype(jnp.int32)
    offsets = touch_ends(jax.random.randint(part_keys[9], (LAYERS,), 1, NB), jax.random.fold_in(part_keys[9], 1), 1, NB - 1).astype(jnp.int32)
    return dict(incident=incident, target=target, down_diag=down_diag, down_off=down_off, up_diag=up_diag, up_off=up_off, design=design, profile=profile, material=material, offsets=offsets)


precise = lax.Precision.HIGHEST


def band_apply(diag_rows, off_rows, shift_by, field_in):
    block_size = diag_rows.shape[1]
    block_count = diag_rows.shape[0] // block_size
    col_width = field_in.shape[1]
    diag_blocks = diag_rows.reshape(block_count, block_size, block_size)
    off_blocks = off_rows.reshape(block_count, block_size, block_size)
    pieces_in = field_in.reshape(block_count, block_size, col_width)
    rolled = jnp.roll(pieces_in, -shift_by, axis=0)
    result = jnp.einsum("ijk,ikw->ijw", diag_blocks, pieces_in, precision=precise)
    result = result + jnp.einsum("ijk,ikw->ijw", off_blocks, rolled, precision=precise)
    return result.reshape(block_count * block_size, col_width)


def band_transpose(diag_rows, off_rows, shift_by, field_in):
    block_size = diag_rows.shape[1]
    block_count = diag_rows.shape[0] // block_size
    col_width = field_in.shape[1]
    diag_blocks = diag_rows.reshape(block_count, block_size, block_size)
    off_blocks = off_rows.reshape(block_count, block_size, block_size)
    pieces_in = field_in.reshape(block_count, block_size, col_width)
    result = jnp.einsum("ikj,ikw->ijw", diag_blocks, pieces_in, precision=precise)
    spread = jnp.einsum("ikj,ikw->ijw", off_blocks, pieces_in, precision=precise)
    result = result + jnp.roll(spread, shift_by, axis=0)
    return result.reshape(block_count * block_size, col_width)


def reference(incident, target, down_diag, down_off, up_diag, up_off, design, profile, material, offsets):
    onehot = (material[:, None] == jnp.arange(profile.shape[0], dtype=jnp.int32)[None, :]).astype(jnp.float32)
    shape_rows = jnp.dot(onehot, profile, precision=precise)
    reflect = design * shape_rows

    def down_step(carried, layer_in):
        diag_rows, off_rows, shift_by = layer_in
        return band_apply(diag_rows, off_rows, shift_by, carried), carried

    _, down_stack = lax.scan(down_step, incident, (down_diag, down_off, offsets))

    def up_step(carried, layer_in):
        diag_rows, off_rows, shift_by, reflect_row, down_here = layer_in
        return reflect_row[:, None] * down_here + band_apply(diag_rows, off_rows, shift_by, carried), None

    reflected, _ = lax.scan(up_step, jnp.zeros_like(incident), (up_diag, up_off, offsets, reflect, down_stack), reverse=True)
    adjoint_start = (reflected - target) / incident.shape[1]

    def adjoint_step(carried, layer_in):
        diag_rows, off_rows, shift_by, down_here = layer_in
        return band_transpose(diag_rows, off_rows, shift_by, carried), jnp.sum(carried * down_here, axis=1)

    _, sums = lax.scan(adjoint_step, adjoint_start, (up_diag, up_off, offsets, down_stack))
    return sums * shape_rows
```

```python
import functools

import jax
import jax.numpy as jnp
from jax import lax
from jax.experimental import pallas as pl
from jax.experimental.pallas import tpu as pltpu
from jax.sharding import PartitionSpec as P

precise = lax.Precision.HIGHEST


def passed_along(value, axis, steps):
    count = lax.axis_size(axis)
    first, last = (max(0, -steps), min(count, count - steps))
    return lax.ppermute(value, axis, [(source, source + steps) for source in range(first, last)])


def band_apply(diag_rows, off_rows, shift_by, field_in):
    block_size = diag_rows.shape[1]
    block_count = diag_rows.shape[0] // block_size
    col_width = field_in.shape[1]
    diag_blocks = diag_rows.reshape(block_count, block_size, block_size)
    off_blocks = off_rows.reshape(block_count, block_size, block_size)
    pieces_in = field_in.reshape(block_count, block_size, col_width)
    rolled = jnp.roll(pieces_in, -shift_by, axis=0)
    result = jnp.einsum("ijk,ikw->ijw", diag_blocks, pieces_in, precision=precise)
    result = result + jnp.einsum("ijk,ikw->ijw", off_blocks, rolled, precision=precise)
    return result.reshape(block_count * block_size, col_width)


def band_transpose(diag_rows, off_rows, shift_by, field_in):
    block_size = diag_rows.shape[1]
    block_count = diag_rows.shape[0] // block_size
    col_width = field_in.shape[1]
    diag_blocks = diag_rows.reshape(block_count, block_size, block_size)
    off_blocks = off_rows.reshape(block_count, block_size, block_size)
    pieces_in = field_in.reshape(block_count, block_size, col_width)
    result = jnp.einsum("ikj,ikw->ijw", diag_blocks, pieces_in, precision=precise)
    spread = jnp.einsum("ikj,ikw->ijw", off_blocks, pieces_in, precision=precise)
    result = result + jnp.roll(spread, shift_by, axis=0)
    return result.reshape(block_count * block_size, col_width)


def run_line(entry_field, local_fn, passer, is_first, turn_count, col_width):

    def one_turn(turn_idx, carried):
        result, _ = local_fn(carried, 0, col_width)
        return jnp.where(is_first, entry_field, passer(result))

    start_field = jnp.where(is_first, entry_field, jnp.zeros_like(entry_field))
    carried = lax.fori_loop(0, turn_count - 1, one_turn, start_field)
    return local_fn(carried, 0, col_width)[1]


def body(
    incident, target, down_diag, down_off, up_diag, up_off, design, profile, material, offsets
):
    columns, aim_cols = (
        lax.all_to_all(incident, "harm", split_axis=1, concat_axis=0, tiled=True),
        lax.all_to_all(target, "harm", split_axis=1, concat_axis=0, tiled=True),
    )
    down_full, down_side, up_full, up_side, design_full = (
        lax.all_gather(down_diag, "harm", axis=1, tiled=True),
        lax.all_gather(down_off, "harm", axis=1, tiled=True),
        lax.all_gather(up_diag, "harm", axis=1, tiled=True),
        lax.all_gather(up_off, "harm", axis=1, tiled=True),
        lax.all_gather(design, "harm", axis=1, tiled=True),
    )
    onehot = (material[:, None] == jnp.arange(profile.shape[0], dtype=jnp.int32)[None, :]).astype(
        jnp.float32
    )
    shape_rows = jnp.dot(onehot, profile, precision=precise)
    reflect = design_full * shape_rows
    col_width = columns.shape[1]
    total_inc = col_width * lax.axis_size("harm")
    layer_count = lax.axis_size("layer")
    where_now = lax.axis_index("layer")

    def down_local(source, col_start, span_width):

        def down_step(carried, layer_in):
            diag_rows, off_rows, shift_by = layer_in
            return (band_apply(diag_rows, off_rows, shift_by, carried), carried)

        result, stacked = lax.scan(down_step, source, (down_full, down_side, offsets))
        return (result, stacked)

    down_stack = run_line(
        columns,
        down_local,
        lambda sent: passed_along(sent, "layer", 1),
        where_now == 0,
        layer_count,
        col_width,
    )

    def up_local(source, col_start, span_width):

        def up_step(carried, layer_in):
            diag_rows, off_rows, shift_by, reflect_row, down_here = layer_in
            return (
                reflect_row[:, None] * down_here
                + band_apply(diag_rows, off_rows, shift_by, carried),
                None,
            )

        result, _ = lax.scan(
            up_step, source, (up_full, up_side, offsets, reflect, down_stack), reverse=True
        )
        return (result, result)

    def adjoint_local(source, col_start, span_width):

        def adjoint_step(carried, layer_in):
            diag_rows, off_rows, shift_by = layer_in
            return (band_transpose(diag_rows, off_rows, shift_by, carried), carried)

        result, stacked = lax.scan(adjoint_step, source, (up_full, up_side, offsets))
        return (result, stacked)

    zero_cols = jnp.zeros_like(columns)
    reflected = run_line(
        zero_cols,
        up_local,
        lambda sent: passed_along(sent, "layer", -1),
        where_now == layer_count - 1,
        layer_count,
        col_width,
    )
    adjoint_start = (reflected - aim_cols) / total_inc
    adjoint_stack = run_line(
        adjoint_start,
        adjoint_local,
        lambda sent: passed_along(sent, "layer", 1),
        where_now == 0,
        layer_count,
        col_width,
    )
    partial_terms = jnp.sum(adjoint_stack * down_stack, axis=2) * shape_rows
    return lax.psum_scatter(partial_terms, "harm", scatter_dimension=1, tiled=True)


CHUNKS = 2
BLOCK = 128
NEAR = {0: 1, 3: 2}
SITES = (1, 2)
ACTIVE = pl.Squeezed()


def moved(value, pairs):
    flat = [(za * 4 + xa * 2 + ca, zb * 4 + xb * 2 + cb) for (za, xa, ca), (zb, xb, cb) in pairs]
    return lax.ppermute(value, ("layer", "harm"), flat)


def split_store(hl, value):
    high = value.astype(jnp.bfloat16)
    hl[:, :BLOCK] = high
    hl[:, BLOCK:] = (value - high.astype(jnp.float32)).astype(jnp.bfloat16)


def three_products(left_high, left_low, right, dims):
    wide = lax.dot_general(left_high, right, dims, preferred_element_type=jnp.float32)
    thin = lax.dot_general(left_low, right[:, :BLOCK], dims, preferred_element_type=jnp.float32)
    return wide[:, :BLOCK] + (wide[:, BLOCK:] + thin)


def block_rows(ref, at):
    return ref[pl.ds(pl.multiple_of(at * BLOCK, BLOCK), BLOCK), :]


def banded(wh, wl, hl, shift, blocks, emit):
    dims = (((1,), (0,)), ((), ()))
    for i in range(blocks):
        j = lax.rem(i + shift, blocks)
        rows = slice(i * BLOCK, (i + 1) * BLOCK)
        right = jnp.concatenate([hl[rows, :], block_rows(hl, j)], axis=0)
        emit(rows, three_products(wh[rows, :], wl[rows, :], right, dims))


def banded_transpose(wh, wl, hl, shift, blocks, emit):
    dims = (((0,), (0,)), ((), ()))
    for j in range(blocks):
        i = lax.rem(j - shift + blocks, blocks)
        rows = slice(j * BLOCK, (j + 1) * BLOCK)
        right = jnp.concatenate([hl[rows, :], block_rows(hl, i)], axis=0)
        high = jnp.concatenate([wh[rows, :BLOCK], block_rows(wh, i)[:, BLOCK:]], axis=0)
        low = jnp.concatenate([wl[rows, :BLOCK], block_rows(wl, i)[:, BLOCK:]], axis=0)
        emit(rows, three_products(high, low, right, dims))


def at_site(s, site, core):
    return (s[0] == site) & (s[1] == core)


def prep_kernel(core, s, *refs):
    pieces, outs = refs[:8], refs[8:]
    wh, wl = outs[0], outs[1]

    @pl.when((s[1] == core) & ((s[0] == 1) | (s[0] == 2)))
    def _():
        inner_base = jnp.where(s[0] == 1, 2, 0)
        for index, piece in enumerate(pieces):
            base = inner_base if index < 4 else 2 - inner_base
            side = s[2] if index % 4 < 2 else 1 - s[2]
            lane = core if index % 2 == 0 else 1 - core
            for l in range(2):
                for r in range(2):
                    top = l * 2 * BLOCK + r * BLOCK
                    block = jnp.concatenate(
                        [piece[top : top + BLOCK, :], piece[4 * BLOCK + top : 5 * BLOCK + top, :]], axis=1
                    )
                    high = block.astype(jnp.bfloat16)
                    low = (block - high.astype(jnp.float32)).astype(jnp.bfloat16)
                    at = side * 4 + lane * 2 + r
                    rows = pl.ds(pl.multiple_of(at * BLOCK, BLOCK), BLOCK)
                    wh[base + l, rows, :] = high
                    wl[base + l, rows, :] = low
                    if len(outs) > 2:
                        row = piece[8 * BLOCK + 2 * l + r : 8 * BLOCK + 2 * l + r + 1, :]
                        outs[2][base + l, rows, :] = jnp.transpose(jnp.broadcast_to(row, (BLOCK, BLOCK)))


def down_kernel(site, blocks, last, s, field, wh, wl, stack, out, cur, hl):
    l = pl.program_id(0)
    steps = pl.num_programs(0)
    active = at_site(s, site, 0)

    @pl.when(active & (l == 0))
    def _():
        cur[...] = field[...]

    @pl.when(active)
    def _():
        value = cur[...]
        stack[...] = value
        split_store(hl, value)

    @pl.when(active & ((l < steps - 1) | last))
    def _():
        def emit(rows, value):
            cur[rows, :] = value

        banded(wh, wl, hl, s[3 + l], blocks, emit)

    @pl.when(active & (l == steps - 1))
    def _():
        out[...] = cur[...]


def up_kernel(site, blocks, top, s, *refs):
    field = None if top else refs[0]
    wh, wl, stack, mirror, out, cur, hl = refs[0 if top else 1 :]
    l = pl.program_id(0)
    steps = pl.num_programs(0)
    active = at_site(s, site, 1)

    @pl.when(active & (l == 0))
    def _():
        cur[...] = jnp.zeros_like(cur) if top else field[...]

    @pl.when(active)
    def _():
        split_store(hl, cur[...])

        def emit(rows, value):
            cur[rows, :] = mirror[rows, :] * stack[rows, :] + value

        banded(wh, wl, hl, s[3 + steps - 1 - l], blocks, emit)

    @pl.when(active & (l == steps - 1))
    def _():
        out[...] = cur[...]


def adjoint_kernel(site, blocks, total, s, *refs):
    first = total is not None
    field = refs[0]
    wh, wl, stack, sums, out, cur, hl = refs[2 if first else 1 :]
    l = pl.program_id(0)
    steps = pl.num_programs(0)
    active = at_site(s, site, 1)

    @pl.when(active & (l == 0))
    def _():
        cur[...] = (field[...] - refs[1][...]) / total if first else field[...]

    @pl.when(active)
    def _():
        split_store(hl, cur[...])
        for i in range(blocks):
            rows = slice(i * BLOCK, (i + 1) * BLOCK)
            terms = jnp.transpose(cur[rows, :] * stack[rows, :])
            sums[i : i + 1, :] = jnp.sum(terms, axis=0, keepdims=True)

    @pl.when(active & ((l < steps - 1) | first))
    def _():
        def emit(rows, value):
            cur[rows, :] = value

        banded_transpose(wh, wl, hl, s[3 + l], blocks, emit)

    @pl.when(active & (l == steps - 1))
    def _():
        out[...] = cur[...]


def call(kernel, scalars, inputs, in_specs, out_shape, out_specs, grid, scratch=()):
    return pl.pallas_call(
        kernel,
        out_shape=out_shape,
        grid_spec=pltpu.PrefetchScalarGridSpec(
            num_scalar_prefetch=1, grid=grid, in_specs=in_specs, out_specs=out_specs, scratch_shapes=list(scratch)
        ),
    )(scalars, *inputs)


def whole(shape):
    return pl.BlockSpec(shape, lambda l, s: (0,) * len(shape))


def layer_block(steps, rows, width, reverse=False):
    index = (lambda l, s: (steps - 1 - l, 0, 0)) if reverse else (lambda l, s: (l, 0, 0))
    return pl.BlockSpec((ACTIVE, rows, width), index)


def fast_body(
    incident, target, down_diag, down_off, up_diag, up_off, design, profile, material, offsets
):
    rows_here, col_total = incident.shape
    harm_total = rows_here * 4
    blocks = harm_total // BLOCK
    steps = 4
    f32 = jnp.float32
    here_z, here_h = lax.axis_index("layer"), lax.axis_index("harm")
    here_x, here_c = here_h // 2, here_h % 2
    onehot = (material[:, None] == jnp.arange(profile.shape[0], dtype=jnp.int32)[None, :]).astype(f32)
    profile_here = lax.dynamic_slice_in_dim(profile, here_h * rows_here, rows_here, 1)
    shape_rows = jnp.dot(onehot, profile_here, precision=precise)
    reflect = design * shape_rows
    extra = jnp.concatenate(
        [
            reflect.reshape(4, BLOCK),
            jnp.broadcast_to(offsets.astype(f32)[:, None], (2, BLOCK)),
            jnp.zeros((2, BLOCK), f32),
        ],
        axis=0,
    )

    def packed(diag, off):
        return jnp.concatenate([diag.reshape(-1, BLOCK), off.reshape(-1, BLOCK), extra], axis=0)

    zs, xs = range(4), range(2)

    def gathered(core, own, swap_from):
        swapped = moved(swap_from, [((z, x, 1 - core), (z, x, core)) for z in zs for x in xs])
        over_x = lambda v, at: moved(v, [((z, x, core), (z, 1 - x, core)) for z in at for x in xs])
        over_z = lambda v: moved(v, [((z, x, core), (n, x, core)) for z, n in NEAR.items() for x in xs])
        if core:
            own, swapped = lax.optimization_barrier((own, swapped))
        beside_a = over_x(own, zs)
        outer_a = over_z(own)
        beside_b = over_x(swapped, SITES)
        outer_b = over_z(swapped)
        outer_beside_a = over_z(beside_a)
        outer_beside_b = over_x(outer_b, SITES)
        return [own, swapped, beside_a, beside_b, outer_a, outer_b, outer_beside_a, outer_beside_b]

    def column_group(value, core, site):
        chunk_cols = col_total // 2 // CHUNKS
        part = lambda x: lax.dynamic_slice_in_dim(value, x * (col_total // 2), col_total // 2, 1)
        cut = lambda v: v.reshape(rows_here, CHUNKS, chunk_cols).transpose(1, 0, 2)
        mine, others = cut(part(here_x)), cut(part(1 - here_x))
        partner = moved(mine, [((site, x, 1 - core), (site, x, core)) for x in xs])
        beside = moved(others, [((site, x, core), (site, 1 - x, core)) for x in xs])
        across = moved(others, [((site, x, 1 - core), (site, 1 - x, core)) for x in xs])
        near = [mine, partner] if core == 0 else [partner, mine]
        far = [beside, across] if core == 0 else [across, beside]
        return jnp.where(here_x == 0, jnp.concatenate(near + far, 1), jnp.concatenate(far + near, 1))

    down_pack = packed(down_diag, down_off)
    up_pack = packed(up_diag, up_off)
    down_pieces = gathered(0, down_pack, down_pack)
    entry = column_group(incident, 0, 1)
    up_pack_later, _ = lax.optimization_barrier((up_pack, down_pieces[5]))
    up_pieces = gathered(1, up_pack, up_pack_later)
    aim = column_group(target, 1, 1)

    def scalars(pieces):
        outer = pieces[4][8 * BLOCK + 4 : 8 * BLOCK + 6, 0].astype(jnp.int32)
        turn = jnp.where(here_z < 2, jnp.concatenate([outer, offsets]), jnp.concatenate([offsets, outer]))
        return jnp.concatenate([jnp.stack([here_z, here_c, here_x]), turn])

    def prepared(core, pieces, scal):
        weight = jax.ShapeDtypeStruct((steps, harm_total, 2 * BLOCK), jnp.bfloat16)
        outs = [weight, weight] + ([jax.ShapeDtypeStruct((steps, harm_total, BLOCK), f32)] if core else [])
        return call(
            functools.partial(prep_kernel, core),
            scal,
            pieces,
            [whole(p.shape) for p in pieces],
            outs,
            [whole(o.shape) for o in outs],
            (1,),
        )

    down_scal, up_scal = scalars(down_pieces), scalars(up_pieces)
    cols = col_total // 2 // CHUNKS
    field_shape = jax.ShapeDtypeStruct((harm_total, cols), f32)
    stack_shape = jax.ShapeDtypeStruct((steps, harm_total, cols), f32)
    field_spec = whole((harm_total, cols))
    scratch = [pltpu.VMEM((harm_total, cols), f32), pltpu.VMEM((harm_total, 2 * cols), jnp.bfloat16)]
    weight_spec = layer_block(steps, harm_total, 2 * BLOCK)
    stack_spec = layer_block(steps, harm_total, cols)
    weight_back = layer_block(steps, harm_total, 2 * BLOCK, True)
    stack_back = layer_block(steps, harm_total, cols, True)
    dh, dl = prepared(0, down_pieces, down_scal)

    def down_pass(site, field, last):
        return call(
            functools.partial(down_kernel, site, blocks, last),
            down_scal,
            [field, dh, dl],
            [field_spec, weight_spec, weight_spec],
            [stack_shape, field_shape],
            [stack_spec, field_spec],
            (steps,),
            scratch,
        )

    to_two = lambda v, core: moved(v, [((1, x, core), (2, x, core)) for x in xs])
    to_one = lambda v, core: moved(v, [((2, x, core), (1, x, core)) for x in xs])
    chunks = range(CHUNKS)
    stacks_one, handed = zip(*[down_pass(1, entry[k], True) for k in chunks])
    received = [to_two(v, 0) for v in handed]
    stacks_two = [down_pass(2, v, False)[0] for v in received]
    share = lambda v, site: moved(v, [((site, x, 0), (site, x, 1)) for x in xs])
    stacks_two = [share(v, 2) for v in stacks_two]
    stacks_one = [share(v, 1) for v in stacks_one]
    uh, ul, mirror = prepared(1, up_pieces, up_scal)

    def up_pass(site, field, stack):
        top = field is None
        return call(
            functools.partial(up_kernel, site, blocks, top),
            up_scal,
            ([] if top else [field]) + [uh, ul, stack, mirror],
            ([] if top else [field_spec]) + [weight_back, weight_back, stack_back, stack_back],
            field_shape,
            field_spec,
            (steps,),
            scratch,
        )

    def adjoint_pass(site, fields, stack, total):
        sums_shape = jax.ShapeDtypeStruct((steps, blocks, BLOCK), f32)
        return call(
            functools.partial(adjoint_kernel, site, blocks, total),
            up_scal,
            fields + [uh, ul, stack],
            [field_spec] * len(fields) + [weight_spec, weight_spec, stack_spec],
            [sums_shape, field_shape],
            [layer_block(steps, blocks, BLOCK), field_spec],
            (steps,),
            scratch,
        )

    risen = [to_one(up_pass(2, None, stacks_two[k]), 1) for k in chunks]
    sums_one, passed = [], []
    for k in chunks:
        reflected = up_pass(1, risen[k], stacks_one[k])
        sums, adjoint = adjoint_pass(1, [reflected, aim[k]], stacks_one[k], float(col_total))
        sums_one.append(sums)
        passed.append(to_two(adjoint, 1))
    sums_two = [adjoint_pass(2, [passed[k]], stacks_two[k], None)[0] for k in chunks]

    half = blocks // 2
    total_of = lambda parts: functools.reduce(jnp.add, parts)
    part_of = lambda v, x: lax.dynamic_slice_in_dim(v, x * half, half, 1)

    def finished(site, sums):
        full = total_of(sums)
        partner = moved(part_of(full, 1 - here_x), [((site, x, 1), (site, 1 - x, 1)) for x in xs])
        mine = part_of(full, here_x) + partner
        outer_at = 0 if site == 1 else 3
        low, high = mine[:2], mine[2:]
        inner, outer = (high, low) if site == 1 else (low, high)
        a = moved(inner[:, :2], [((site, x, 1), (site, x, 0)) for x in xs])
        b = moved(outer[:, :2], [((site, x, 1), (outer_at, x, 0)) for x in xs])
        c = moved(outer[:, 2:], [((site, x, 1), (outer_at, x, 1)) for x in xs])
        kept = jnp.where((here_z == site) & (here_c == 1), inner[:, 2:], 0.0)
        return a + b + (c + kept)

    total = finished(1, sums_one) + finished(2, sums_two)
    return total.reshape(2, rows_here) * shape_rows


def takes_fast_plan(mesh):
    return mesh.shape["layer"] == 4 and mesh.shape["harm"] == 4


def solution(mesh):
    return jax.shard_map(
        fast_body if takes_fast_plan(mesh) else body,
        mesh=mesh,
        in_specs=(
            P(("design", "harm"), None),
            P(("design", "harm"), None),
            P(("design", "layer"), "harm", None),
            P(("design", "layer"), "harm", None),
            P(("design", "layer"), "harm", None),
            P(("design", "layer"), "harm", None),
            P(("design", "layer"), "harm"),
            P(),
            P(("design", "layer")),
            P(("design", "layer")),
        ),
        out_specs=P(("design", "layer"), "harm"),
        check_vma=False,
    )
```
